256 devices in a mesh: dm: 32 (over y, x, z_lo), chan: 8 (over z_hi, core).
Axes of the slice: x: 4, y: 4, z: 8 (z_hi: 4, z_lo: 2; z = z_hi * 2 + z_lo), core: 2. Of those that a mesh axis runs over, the one named last changes fastest.
Arguments:
- phased: bfloat16 [32, 256, 2, 4096], P('dm', None, None, 'chan')
- filters: bfloat16 [64, 4096, 512], P('dm', 'chan'), may hold values from -0.375 to 0.375
- tap_blocks: int32 [64], replicated, may hold values from 1 to 4, as said below
- stretch_owner: int32 [4], replicated, may hold values from 0 to 31, as said below
Outputs:
- normalized_power: float32 [64, 64, 4096], P('dm', None, 'chan')
The draws below stay inside these ranges and needn't reach their ends.
Inputs may be any that keep to these rules, and one draw needn't show every extreme that they name: `stretch_owner`: the owners of the 4 stretches are distinct slots. `tap_blocks`: never falls from one trial to the next.
All inputs are finite; a program needn't handle non-finite values.
Results may differ from the reference program's by a relative error of at most 0.0003.
Values may be sent and summed in bfloat16 or wider, within the bound.
No kernel may reach another device: no remote copies, remote signals or barrier semaphores. Data moves between devices by JAX's collectives and lax.ppermute only.
A program may use at most 128 MiB of HBM per device.

```python
import jax
import jax.numpy as jnp
from jax import lax

CHANS = 4096
TAPS = 256
BLOCK = 64
SAMPLES = 256
STRETCHES = 4
DOWN = 16
TRIALS = 64
SLOTS = 32
NBLOCKS = 4


def draw_phased(key, part):
    first, second = jax.random.split(key, 2)
    position = jnp.arange(CHANS, dtype=jnp.float32) / CHANS
    rough = jnp.exp(jax.random.uniform(second, (CHANS,), jnp.float32, -0.35, 0.35))
    amplitude = jnp.sqrt(10.0 ** position) * rough
    values = amplitude * jax.random.truncated_normal(first, -6.0, 6.0, (SLOTS, SAMPLES, 2, CHANS), jnp.float32)
    return values.astype(jnp.bfloat16)


def draw_tap_blocks(key, part):
    counts = jax.random.randint(key, (TRIALS,), 0, NBLOCKS)
    counts = jnp.sort(counts)
    counts = counts.at[0].set(0).at[TRIALS - 1].set(NBLOCKS - 1)
    return (counts + 1).astype(jnp.int32)


def draw_stretch_owner(key, part):
    first, second = jax.random.split(key)
    picked = jax.random.permutation(first, SLOTS - 1)[:STRETCHES]
    where_last = jax.random.randint(second, (), 0, STRETCHES)
    picked = jnp.where(jnp.arange(STRETCHES) == where_last, SLOTS - 1, picked)
    return picked.astype(jnp.int32)


def block_scale(stream_key, dims, cuts, least, high):
    level = 1.0
    for dim, shards_of in cuts:
        steps = jax.random.uniform(jax.random.fold_in(jax.random.fold_in(stream_key, 6), dim), (shards_of,), jnp.float32, least / len(cuts), high / len(cuts))
        level = level * jnp.repeat(jnp.exp(steps), dims[dim] // shards_of).reshape((-1,) + (1,) * (len(dims) - 1 - dim))
    return level


def scatter_about(own_key, shape, scale, bound, shards=(), kind=jnp.bfloat16):
    array = scale * jax.random.normal(own_key, shape, jnp.float32)
    if shards:
        array = array * block_scale(own_key, shape, shards, -0.22, 0.18)
    return jnp.clip(array, -bound, bound).astype(kind)


def setup_inputs(seed: int = 0) -> dict:
    keys = jax.random.split(jax.random.key(seed), 5)
    return {
        "phased": draw_phased(jax.random.fold_in(keys[4], 71), 0),
        "filters": scatter_about(keys[1], (TRIALS, CHANS, 2 * TAPS), TAPS ** -0.5, 0.375, ((0, 32), (1, 8))),
        "tap_blocks": draw_tap_blocks(jax.random.fold_in(keys[4], 71), 0),
        "stretch_owner": draw_stretch_owner(jax.random.fold_in(keys[4], 71), 0),
    }


epsilon = 1e-6


def reference(phased, filters, tap_blocks, stretch_owner):
    stretch_list = [lax.dynamic_index_in_dim(phased, stretch_owner[k], 0, keepdims=False) for k in range(STRETCHES)]
    signal = jnp.concatenate([jnp.zeros((TAPS, 2, CHANS), phased.dtype)] + stretch_list, axis=0).astype(jnp.float32)
    tap_index = jnp.arange(TAPS, dtype=jnp.int32)
    live = tap_index[None, :] < (tap_blocks * BLOCK)[:, None]
    live_both = jnp.concatenate([live, live], axis=1).astype(jnp.float32)
    taps_full = filters.astype(jnp.float32) * live_both[:, None, :]
    lag_index = TAPS + jnp.arange(SAMPLES, dtype=jnp.int32)[None, :] - tap_index[:, None]
    block_width = min(128, CHANS)
    outputs = []
    for k in range(STRETCHES):
        segment = signal[k * SAMPLES: k * SAMPLES + TAPS + SAMPLES]

        def per_block(index):
            first = (index * block_width).astype(jnp.int32)
            section = lax.dynamic_slice_in_dim(segment, first, block_width, axis=2)
            lagged = section[lag_index]
            real_part = lagged[:, :, 0, :]
            imag_part = lagged[:, :, 1, :]
            upper = jnp.concatenate([real_part, imag_part], axis=1)
            lower = jnp.concatenate([-imag_part, real_part], axis=1)
            toeplitz = jnp.concatenate([upper, lower], axis=0)
            tap_slab = lax.dynamic_slice_in_dim(taps_full, first, block_width, axis=1)
            filtered = jnp.einsum("twm,mnw->twn", tap_slab, toeplitz, precision=lax.Precision.HIGHEST)
            real_out = filtered[:, :, :SAMPLES]
            imag_out = filtered[:, :, SAMPLES:]
            energy = real_out * real_out + imag_out * imag_out
            return jnp.sum(energy.reshape(TRIALS, block_width, SAMPLES // DOWN, DOWN), axis=3) / DOWN

        blocks = lax.map(per_block, jnp.arange(CHANS // block_width, dtype=jnp.int32))
        outputs.append(blocks.transpose(1, 3, 0, 2).reshape(TRIALS, SAMPLES // DOWN, CHANS))
    detected = jnp.concatenate(outputs, axis=1)
    band = jnp.sum(detected, axis=2) / CHANS
    return detected / (band[:, :, None] + epsilon)
```

```python
import functools

import jax
import jax.numpy as jnp
import numpy as np
from jax import lax
from jax.experimental import pallas as pl
from jax.experimental.pallas import tpu as pltpu
from jax.sharding import PartitionSpec as P

CHANS = 4096
BLOCK = 64
DOWN = 16
HALF = 256
NC = 16
GROUP = 2
DM = 32

epsilon = 1e-06


def place(i):
    return i // 8, (i // 2) % 4, i % 2


def index(y, x, z):
    return ((y % 4) * 4 + x % 4) * 2 + z % 2


def hop(value, dy, dx, dz):
    pairs = []
    for i in range(DM):
        y, x, z = place(i)
        pairs.append((i, index(y + dy, x + dx, z + dz)))
    return lax.ppermute(value, "dm", pairs)


def time_order():
    table = np.zeros((512,), np.int32)
    for bh in range(2):
        for ri in range(2):
            for bl in range(8):
                for m in range(16):
                    k = ((bh * 2 + ri) * 8 + bl) * 16 + m
                    table[k] = (16 * m + 15 - (8 * bh + bl)) * 2 + ri
    return table


def piece_table():
    rows = []
    for i in range(DM):
        y, x, _ = place(i)
        row = []
        for dy in (0, -1, 1, 2):
            for dx in (0, -1, 1, 2):
                row.append(4 * ((y + dy) % 4) + (x + dx) % 4)
        rows.append(row)
    return np.array(rows, np.int32)


TAP_CH = 16


def tap_kernel(width_ref, f_ref, o_ref):
    lane = lax.broadcasted_iota(jnp.int32, (16, 128), 1)
    row = lax.broadcasted_iota(jnp.int32, (16, 128), 0)
    keep = lane >= row

    def group(step, carry):
        at = pl.multiple_of(step * TAP_CH, TAP_CH)
        for t in range(2):
            live = width_ref[t]
            for h in range(2):
                block = f_ref[t, pl.ds(at, TAP_CH), 256 * h : 256 * h + 256].astype(jnp.float32)
                tap = lax.broadcasted_iota(jnp.int32, block.shape, 1)
                block = jnp.where(tap < live, block, 0.0)
                base = (t * 2 + h) * 16
                for c in range(TAP_CH):
                    low = jnp.broadcast_to(block[c : c + 1, :128], (16, 128))
                    high = jnp.broadcast_to(block[c : c + 1, 128:], (16, 128))
                    low = pltpu.roll(low, 0, 1, stride=1, stride_axis=0)
                    high = pltpu.roll(high, 0, 1, stride=1, stride_axis=0)
                    rows = slice(base, base + 16)
                    o_ref[at + c, rows, 0:128] = jnp.where(keep, low, 0.0).astype(jnp.bfloat16)
                    o_ref[at + c, rows, 128:256] = jnp.where(keep, high, low).astype(jnp.bfloat16)
                    o_ref[at + c, rows, 256:384] = jnp.where(keep, 0.0, high).astype(jnp.bfloat16)
        return carry

    lax.fori_loop(0, HALF // TAP_CH, group, 0)


def in_vmem():
    return pl.BlockSpec(memory_space=pltpu.VMEM)


def in_smem():
    return pl.BlockSpec(memory_space=pltpu.SMEM)


def build_taps(widths, taps):
    return pl.pallas_call(
        tap_kernel,
        in_specs=[in_smem(), in_vmem()],
        out_specs=in_vmem(),
        out_shape=jax.ShapeDtypeStruct((HALF, 64, 384), jnp.bfloat16),
        cost_estimate=pl.CostEstimate(flops=10_000_000, bytes_accessed=14_000_000, transcendentals=0),
        compiler_params=pltpu.CompilerParams(vmem_limit_bytes=16 << 20),
        name="build_taps",
    )(widths, taps)


def assemble_kernel(own_ref, x_ref, o_ref, scr):
    lane = lax.broadcasted_iota(jnp.int32, (16, 128), 1) // 16
    for bh in range(2):
        held = []
        for ri in range(2):
            for k in range(4):
                at = 256 * bh + 128 * ri
                held.append(x_ref[own_ref[k], :, at : at + 128].astype(jnp.float32))
        for k in (4, 2, 1):
            low = (lane & k) == 0
            for p in range(8):
                if p & k:
                    continue
                a, b = held[p], held[p + k]
                held[p] = jnp.where(low, a, pltpu.roll(b, 16 * k, 1))
                held[p + k] = jnp.where(low, pltpu.roll(a, 128 - 16 * k, 1), b)
        for bl in range(8):
            scr[pl.ds(8 * bh + bl, 16, stride=16), :] = held[bl]
    o_ref[...] = scr[...].reshape(16, 16, 128).astype(jnp.bfloat16)


def assemble(owner, arrived):
    return pl.pallas_call(
        assemble_kernel,
        in_specs=[in_smem(), in_vmem()],
        out_specs=in_vmem(),
        out_shape=jax.ShapeDtypeStruct((16, 16, 128), jnp.bfloat16),
        scratch_shapes=[pltpu.VMEM((256, 128), jnp.float32)],
        compiler_params=pltpu.CompilerParams(vmem_limit_bytes=16 << 20),
        name="assemble",
    )(owner, arrived)


def fold(rows):
    sub = lax.broadcasted_iota(jnp.int32, (8, 128), 0)
    for k in (4, 2, 1):
        low = (sub & k) == 0
        rows = [
            jnp.where(low, rows[i], rows[i + k])
            + jnp.where(low, pltpu.roll(rows[i], 8 - k, 0), pltpu.roll(rows[i + k], k, 0))
            for i in range(k)
        ]
    return rows[0]


def detect_kernel(counts, piece_ref, t0_ref, t1_ref, *rest):
    d_ref, b_ref, w_scr = rest[-3:]
    lane = lax.broadcasted_iota(jnp.int32, (16, 128), 1)
    inner = lane % 64
    sign = jnp.where(lane < 64, -1.0, 1.0)
    b_ref[...] = jnp.zeros_like(b_ref)

    def group(x_ref, first, step, carry):
        for p in range(GROUP):
            source = (step * GROUP + p) * NC
            base = pl.multiple_of(piece_ref[first + step * GROUP + p] * NC, NC)
            sums = [[] for _ in range(4)]
            for c in range(NC):
                x = x_ref[source + c]
                slot = p * NC + c
                w_scr[slot, 0:16, :] = x
                for a in range(1, 17):
                    moved = pltpu.roll(x, a, 1)
                    w_scr[slot, 16 * a : 16 * a + 16, :] = jnp.where(inner >= a, moved, jnp.zeros_like(x))
                taps = jnp.concatenate([t0_ref[base + c, :, :272], t1_ref[base + c, :, :272]], axis=0)
                out = jnp.dot(taps, w_scr[slot], preferred_element_type=jnp.float32)
                for t in range(4):
                    real = out[32 * t : 32 * t + 16]
                    imag = out[32 * t + 16 : 32 * t + 32]
                    y = real + sign * pltpu.roll(imag, 64, 1)
                    y = y * y
                    sums[t].append(y[:8] + y[8:])
            for t in range(4):
                for g in range(0, NC, 8):
                    total = fold(sums[t][g : g + 8])
                    total = (total + pltpu.roll(total, 64, 1)) * (1.0 / DOWN)
                    d_ref[t, pl.ds(base + g, 8)] = total
                    b_ref[t] += total
        return carry

    first = 0
    for x_ref, count in zip(rest, counts):
        lax.fori_loop(0, count // GROUP, functools.partial(group, x_ref, first), 0)
        first += count


def detect(pieces, samples, taps, earlier=None):
    counts = [part.shape[0] // NC for part in samples]
    n = sum(counts) * NC
    in_specs = [in_smem()] + [in_vmem()] * (2 + len(samples))
    args = [pieces, *taps, *samples]
    aliases = {}
    if earlier is not None:
        in_specs.append(in_vmem())
        args.append(earlier)
        aliases = {len(args) - 1: 0}
    return pl.pallas_call(
        functools.partial(detect_kernel, counts),
        in_specs=in_specs,
        out_specs=[in_vmem(), in_vmem()],
        out_shape=[
            jax.ShapeDtypeStruct((4, HALF, 128), jnp.float32),
            jax.ShapeDtypeStruct((4, 8, 128), jnp.float32),
        ],
        scratch_shapes=[pltpu.VMEM((GROUP * NC, 272, 128), jnp.bfloat16)],
        input_output_aliases=aliases,
        cost_estimate=pl.CostEstimate(
            flops=n * 128 * 512 * 128 * 2, bytes_accessed=n * 128 * 384 * 2, transcendentals=0
        ),
        compiler_params=pltpu.CompilerParams(vmem_limit_bytes=16 << 20),
        name="detect",
    )(*args)


def turn_kernel(d_ref, o_ref):
    for t in range(4):
        o_ref[t] = d_ref[t].T[:64]


def turn(detected):
    return pl.pallas_call(
        turn_kernel,
        in_specs=[in_vmem()],
        out_specs=in_vmem(),
        out_shape=jax.ShapeDtypeStruct((4, 64, HALF), jnp.float32),
        compiler_params=pltpu.CompilerParams(vmem_limit_bytes=16 << 20),
        name="turn",
    )(detected)


def body(phased, filters, tap_blocks, stretch_owner):
    me = lax.axis_index("dm")
    z = me % 2
    widths = tap_blocks * BLOCK
    mine = lax.dynamic_slice_in_dim(widths, me * 2, 2)
    partner = lax.dynamic_slice_in_dim(widths, (me + 1 - 2 * z) * 2, 2)
    pieces = lax.dynamic_index_in_dim(jnp.asarray(piece_table()), me, 0, keepdims=False)

    away = lax.dynamic_slice_in_dim(filters, (1 - z) * HALF, HALF, axis=1)
    partner_taps = hop(away, 0, 0, 1)
    stay = lax.dynamic_slice_in_dim(filters, z * HALF, HALF, axis=1)

    source = lax.broadcasted_iota(jnp.int32, (256, 2, 512), 0) * 2 + lax.broadcasted_iota(jnp.int32, (256, 2, 512), 1)
    order = (source == jnp.asarray(time_order())[None, None, :]).astype(jnp.bfloat16)
    held = jnp.einsum("trc,trk->ck", phased[0], order, preferred_element_type=jnp.float32).astype(jnp.bfloat16)
    sent = held.reshape(2, DM // 2, 16, 512).transpose(1, 0, 2, 3).reshape(DM, 16, 512)
    arrived = lax.all_to_all(sent, "dm", 0, 0, tiled=True)

    near = assemble(jnp.clip(stretch_owner, 0, DM - 1), arrived)
    stay, near = lax.optimization_barrier((stay, near))
    line = [hop(near, 0, k, 0) for k in (1, -1, 2)]
    taps0 = build_taps(mine, stay)
    taps0, *line = lax.optimization_barrier((taps0, *line))
    row = jnp.concatenate([near, *line], axis=0)
    taps = (taps0, build_taps(partner, partner_taps))
    low, high, far = hop(row, 1, 0, 0), hop(row, -1, 0, 0), hop(row, 2, 0, 0)

    detected, band0 = detect(pieces[:4], [row], taps)
    detected, band1 = detect(pieces[4:12], [low, high], taps, detected)
    detected, band2 = detect(pieces[12:], [far], taps, detected)

    band = jnp.sum(band0 + band1 + band2, axis=1)[:, :64]
    total = band[:2] + hop(band[2:], 0, 0, 1)
    turned = turn(detected)
    total, turned = lax.optimization_barrier((total, turned))
    other = hop(turned[2:], 0, 0, 1)
    total = total + lax.ppermute(total, "chan", [(i, i ^ 1) for i in range(8)])
    total, other = lax.optimization_barrier((total, other))
    total = total + lax.ppermute(total, "chan", [(i, i ^ 2) for i in range(8)])
    total = total + lax.ppermute(total, "chan", [(i, (6 - i // 2 * 2) + i % 2) for i in range(8)])

    own = turned[:2]
    low = jnp.where(z == 0, own, other)
    high = jnp.where(z == 0, other, own)
    power = jnp.concatenate([low, high], axis=2)
    return power / (total[:, :, None] / CHANS + epsilon)


def solution(mesh):
    in_specs = (P("dm", None, None, "chan"), P("dm", "chan", None), P(), P())
    out_specs = P("dm", None, "chan")
    return jax.shard_map(body, mesh=mesh, in_specs=in_specs, out_specs=out_specs, check_vma=False)
```

```python
import functools

import jax
import jax.numpy as jnp
import numpy as np
from jax import lax
from jax.experimental import pallas as pl
from jax.experimental.pallas import tpu as pltpu
from jax.sharding import PartitionSpec as P

CHANS = 4096
BLOCK = 64
DOWN = 16
HALF = 256
NC = 16
GROUP = 4
DM = 32

epsilon = 1e-06


def place(i):
    return i // 8, (i // 2) % 4, i % 2


def index(y, x, z):
    return ((y % 4) * 4 + x % 4) * 2 + z % 2


def hop(value, dy, dx, dz):
    pairs = []
    for i in range(DM):
        y, x, z = place(i)
        pairs.append((i, index(y + dy, x + dx, z + dz)))
    return lax.ppermute(value, "dm", pairs)


def time_order():
    table = np.zeros((512,), np.int32)
    for bh in range(2):
        for ri in range(2):
            for bl in range(8):
                for m in range(16):
                    k = ((bh * 2 + ri) * 8 + bl) * 16 + m
                    table[k] = (16 * m + 15 - (8 * bh + bl)) * 2 + ri
    return table


def piece_table():
    rows = []
    for i in range(DM):
        y, x, _ = place(i)
        row = []
        for dy in (0, -1, 1, 2):
            for dx in (0, -1, 1, 2):
                row.append(4 * ((y + dy) % 4) + (x + dx) % 4)
        rows.append(row)
    return np.array(rows, np.int32)


TAP_CH = 32


def tap_kernel(live_ref, f_ref, o_ref, scr):
    lane = lax.broadcasted_iota(jnp.int32, (16, 128), 1)
    row = lax.broadcasted_iota(jnp.int32, (16, 128), 0)
    keep = lane >= row

    def group(step, carry):
        at = pl.multiple_of(step * TAP_CH, TAP_CH)
        for t in range(2):
            block = f_ref[t, pl.ds(at, TAP_CH)].astype(jnp.float32)
            tap = lax.broadcasted_iota(jnp.int32, block.shape, 1) % 256
            block = jnp.where(tap < live_ref[t], block, 0.0)
            for k in range(4):
                scr[4 * t + k] = block[:, 128 * k : 128 * k + 128]
        for t in range(2):
            for h in range(2):
                base = (t * 2 + h) * 16
                rows = slice(base, base + 16)
                for c in range(TAP_CH):
                    low = scr[4 * t + 2 * h, pl.ds(c, 16, stride=0)]
                    high = scr[4 * t + 2 * h + 1, pl.ds(c, 16, stride=0)]
                    low = pltpu.roll(low, 0, 1, stride=1, stride_axis=0)
                    high = pltpu.roll(high, 0, 1, stride=1, stride_axis=0)
                    o_ref[at + c, rows, 0:128] = jnp.where(keep, low, 0.0).astype(jnp.bfloat16)
                    o_ref[at + c, rows, 128:256] = jnp.where(keep, high, low).astype(jnp.bfloat16)
                    o_ref[at + c, rows, 256:384] = jnp.where(keep, 0.0, high).astype(jnp.bfloat16)
        return carry

    lax.fori_loop(0, HALF // TAP_CH, group, 0)


def in_vmem():
    return pl.BlockSpec(memory_space=pltpu.VMEM)


def in_smem():
    return pl.BlockSpec(memory_space=pltpu.SMEM)


def build_taps(widths, taps):
    return pl.pallas_call(
        tap_kernel,
        in_specs=[in_smem(), in_vmem()],
        out_specs=in_vmem(),
        out_shape=jax.ShapeDtypeStruct((HALF, 64, 384), jnp.bfloat16),
        scratch_shapes=[pltpu.VMEM((8, TAP_CH, 128), jnp.float32)],
        cost_estimate=pl.CostEstimate(flops=10_000_000, bytes_accessed=14_000_000, transcendentals=0),
        compiler_params=pltpu.CompilerParams(vmem_limit_bytes=16 << 20),
        name="build_taps",
    )(widths, taps)


def assemble_kernel(own_ref, x_ref, o_ref, scr):
    lane = lax.broadcasted_iota(jnp.int32, (16, 128), 1) // 16
    for bh in range(2):
        held = []
        for ri in range(2):
            for k in range(4):
                at = 256 * bh + 128 * ri
                held.append(x_ref[own_ref[k], :, at : at + 128].astype(jnp.float32))
        for k in (4, 2, 1):
            low = (lane & k) == 0
            for p in range(8):
                if p & k:
                    continue
                a, b = held[p], held[p + k]
                held[p] = jnp.where(low, a, pltpu.roll(b, 16 * k, 1))
                held[p + k] = jnp.where(low, pltpu.roll(a, 128 - 16 * k, 1), b)
        for bl in range(8):
            scr[pl.ds(8 * bh + bl, 16, stride=16), :] = held[bl]
    o_ref[...] = scr[...].reshape(16, 16, 128).astype(jnp.bfloat16)


def assemble(owner, arrived):
    return pl.pallas_call(
        assemble_kernel,
        in_specs=[in_smem(), in_vmem()],
        out_specs=in_vmem(),
        out_shape=jax.ShapeDtypeStruct((16, 16, 128), jnp.bfloat16),
        scratch_shapes=[pltpu.VMEM((256, 128), jnp.float32)],
        compiler_params=pltpu.CompilerParams(vmem_limit_bytes=16 << 20),
        name="assemble",
    )(owner, arrived)


def fold(rows):
    sub = lax.broadcasted_iota(jnp.int32, (8, 128), 0)
    for k in (4, 2, 1):
        low = (sub & k) == 0
        rows = [
            jnp.where(low, rows[i], rows[i + k])
            + jnp.where(low, pltpu.roll(rows[i], 8 - k, 0), pltpu.roll(rows[i + k], k, 0))
            for i in range(k)
        ]
    return rows[0]


def detect_kernel(count, piece_ref, t0_ref, t1_ref, x_ref, *rest):
    d_ref, b_ref, w_scr = rest[-3:]
    lane = lax.broadcasted_iota(jnp.int32, (16, 128), 1)
    inner = lane % 64
    sign = jnp.where(lane < 64, -1.0, 1.0)
    b_ref[...] = jnp.zeros_like(b_ref)

    def group(step, carry):
        for p in range(GROUP):
            source = (step * GROUP + p) * NC
            base = pl.multiple_of(piece_ref[step * GROUP + p] * NC, NC)
            sums = [[] for _ in range(4)]
            for c in range(NC):
                x = x_ref[source + c]
                slot = p * NC + c
                w_scr[slot, 0:16, :] = x
                for a in range(1, 17):
                    moved = pltpu.roll(x, a, 1)
                    w_scr[slot, 16 * a : 16 * a + 16, :] = jnp.where(inner >= a, moved, jnp.zeros_like(x))
                taps = jnp.concatenate([t0_ref[base + c, :, :272], t1_ref[base + c, :, :272]], axis=0)
                out = jnp.dot(taps, w_scr[slot], preferred_element_type=jnp.float32)
                for t in range(4):
                    real = out[32 * t : 32 * t + 16]
                    imag = out[32 * t + 16 : 32 * t + 32]
                    y = real + sign * pltpu.roll(imag, 64, 1)
                    y = y * y
                    sums[t].append(y[:8] + y[8:])
            for t in range(4):
                for g in range(0, NC, 8):
                    total = fold(sums[t][g : g + 8])
                    total = (total + pltpu.roll(total, 64, 1)) * (1.0 / DOWN)
                    d_ref[t, pl.ds(base + g, 8)] = total
                    b_ref[t] += total
        return carry

    lax.fori_loop(0, count // GROUP, group, 0)


def detect(pieces, samples, taps, earlier=None):
    n = samples.shape[0]
    in_specs = [in_smem()] + [in_vmem()] * 3
    args = [pieces, *taps, samples]
    aliases = {}
    if earlier is not None:
        in_specs.append(in_vmem())
        args.append(earlier)
        aliases = {len(args) - 1: 0}
    return pl.pallas_call(
        functools.partial(detect_kernel, n // NC),
        in_specs=in_specs,
        out_specs=[in_vmem(), in_vmem()],
        out_shape=[
            jax.ShapeDtypeStruct((4, HALF, 128), jnp.float32),
            jax.ShapeDtypeStruct((4, 8, 128), jnp.float32),
        ],
        scratch_shapes=[pltpu.VMEM((GROUP * NC, 272, 128), jnp.bfloat16)],
        input_output_aliases=aliases,
        cost_estimate=pl.CostEstimate(
            flops=n * 128 * 512 * 128 * 2, bytes_accessed=n * 128 * 384 * 2, transcendentals=0
        ),
        compiler_params=pltpu.CompilerParams(vmem_limit_bytes=16 << 20),
        name="detect",
    )(*args)


def turn_kernel(d_ref, o_ref):
    for t in range(4):
        o_ref[t] = d_ref[t].T[:64]


def turn(detected):
    return pl.pallas_call(
        turn_kernel,
        in_specs=[in_vmem()],
        out_specs=in_vmem(),
        out_shape=jax.ShapeDtypeStruct((4, 64, HALF), jnp.float32),
        compiler_params=pltpu.CompilerParams(vmem_limit_bytes=16 << 20),
        name="turn",
    )(detected)


def body(phased, filters, tap_blocks, stretch_owner):
    me = lax.axis_index("dm")
    z = me % 2
    widths = tap_blocks * BLOCK
    mine = lax.dynamic_slice_in_dim(widths, me * 2, 2)
    partner = lax.dynamic_slice_in_dim(widths, (me + 1 - 2 * z) * 2, 2)
    pieces = lax.dynamic_index_in_dim(jnp.asarray(piece_table()), me, 0, keepdims=False)

    away = lax.dynamic_slice_in_dim(filters, (1 - z) * HALF, HALF, axis=1)
    partner_taps = hop(away, 0, 0, 1)
    stay = lax.dynamic_slice_in_dim(filters, z * HALF, HALF, axis=1)

    source = lax.broadcasted_iota(jnp.int32, (256, 2, 512), 0) * 2 + lax.broadcasted_iota(jnp.int32, (256, 2, 512), 1)
    order = (source == jnp.asarray(time_order())[None, None, :]).astype(jnp.bfloat16)
    held = jnp.einsum("trc,trk->ck", phased[0], order, preferred_element_type=jnp.float32).astype(jnp.bfloat16)
    sent = held.reshape(2, DM // 2, 16, 512).transpose(1, 0, 2, 3).reshape(DM, 16, 512)
    arrived = lax.all_to_all(sent, "dm", 0, 0, tiled=True)

    near = assemble(jnp.clip(stretch_owner, 0, DM - 1), arrived)
    stay, near = lax.optimization_barrier((stay, near))
    line = [hop(near, 0, k, 0) for k in (1, -1, 2)]
    taps0 = build_taps(mine, stay)
    taps0, line = lax.optimization_barrier((taps0, line))
    taps = (taps0, build_taps(partner, partner_taps))
    row = jnp.concatenate([near, *line], axis=0)
    low, high, far = hop(row, 1, 0, 0), hop(row, -1, 0, 0), hop(row, 2, 0, 0)

    detected, bands = None, []
    for step, part in enumerate((row, low, high, far)):
        detected, band = detect(pieces[4 * step : 4 * step + 4], part, taps, detected)
        bands.append(band)

    band = jnp.sum(sum(bands), axis=1)[:, :64]
    total = band[:2] + hop(band[2:], 0, 0, 1)
    turned = turn(detected)
    total, turned = lax.optimization_barrier((total, turned))
    other = hop(turned[2:], 0, 0, 1)
    total = total + lax.ppermute(total, "chan", [(i, i ^ 1) for i in range(8)])
    total = total + lax.ppermute(total, "chan", [(i, i ^ 2) for i in range(8)])
    total, other = lax.optimization_barrier((total, other))
    total = total + lax.ppermute(total, "chan", [(i, (6 - i // 2 * 2) + i % 2) for i in range(8)])

    own = turned[:2]
    low = jnp.where(z == 0, own, other)
    high = jnp.where(z == 0, other, own)
    power = jnp.concatenate([low, high], axis=2)
    return power / (total[:, :, None] / CHANS + epsilon)


def solution(mesh):
    in_specs = (P("dm", None, None, "chan"), P("dm", "chan", None), P(), P())
    out_specs = P("dm", None, "chan")
    return jax.shard_map(body, mesh=mesh, in_specs=in_specs, out_specs=out_specs, check_vma=False)
```

```python
import functools

import jax
import jax.numpy as jnp
import numpy as np
from jax import lax
from jax.experimental import pallas as pl
from jax.experimental.pallas import tpu as pltpu
from jax.sharding import PartitionSpec as P

CHANS = 4096
BLOCK = 64
DOWN = 16
HALF = 256
NC = 16
GROUP = 4
DM = 32

epsilon = 1e-06


def place(i):
    return i // 8, (i // 2) % 4, i % 2


def index(y, x, z):
    return ((y % 4) * 4 + x % 4) * 2 + z % 2


def hop(value, dy, dx, dz):
    pairs = []
    for i in range(DM):
        y, x, z = place(i)
        pairs.append((i, index(y + dy, x + dx, z + dz)))
    return lax.ppermute(value, "dm", pairs)


def time_order():
    table = np.zeros((512,), np.int32)
    for bh in range(2):
        for ri in range(2):
            for bl in range(8):
                for m in range(16):
                    k = ((bh * 2 + ri) * 8 + bl) * 16 + m
                    table[k] = (16 * m + 15 - (8 * bh + bl)) * 2 + ri
    return table


def piece_table():
    rows = []
    for i in range(DM):
        y, x, _ = place(i)
        row = []
        for dy in (0, -1, 1, 2):
            for dx in (0, 2, -1, 1):
                row.append(4 * ((y + dy) % 4) + (x + dx) % 4)
        rows.append(row)
    return np.array(rows, np.int32)


TAP_CH = 32


def tap_kernel(live_ref, f_ref, o_ref, scr):
    lane = lax.broadcasted_iota(jnp.int32, (16, 128), 1)
    row = lax.broadcasted_iota(jnp.int32, (16, 128), 0)
    keep = lane >= row

    def group(step, carry):
        at = pl.multiple_of(step * TAP_CH, TAP_CH)
        for t in range(2):
            block = f_ref[t, pl.ds(at, TAP_CH)].astype(jnp.float32)
            tap = lax.broadcasted_iota(jnp.int32, block.shape, 1) % 256
            block = jnp.where(tap < live_ref[t], block, 0.0)
            for k in range(4):
                scr[4 * t + k] = block[:, 128 * k : 128 * k + 128]
        for t in range(2):
            for h in range(2):
                base = (t * 2 + h) * 16
                rows = slice(base, base + 16)
                for c in range(TAP_CH):
                    low = scr[4 * t + 2 * h, pl.ds(c, 16, stride=0)]
                    high = scr[4 * t + 2 * h + 1, pl.ds(c, 16, stride=0)]
                    low = pltpu.roll(low, 0, 1, stride=1, stride_axis=0)
                    high = pltpu.roll(high, 0, 1, stride=1, stride_axis=0)
                    o_ref[at + c, rows, 0:128] = jnp.where(keep, low, 0.0).astype(jnp.bfloat16)
                    o_ref[at + c, rows, 128:256] = jnp.where(keep, high, low).astype(jnp.bfloat16)
                    o_ref[at + c, rows, 256:384] = jnp.where(keep, 0.0, high).astype(jnp.bfloat16)
        return carry

    lax.fori_loop(0, HALF // TAP_CH, group, 0)


def in_vmem():
    return pl.BlockSpec(memory_space=pltpu.VMEM)


def in_smem():
    return pl.BlockSpec(memory_space=pltpu.SMEM)


def build_taps(widths, taps):
    return pl.pallas_call(
        tap_kernel,
        in_specs=[in_smem(), in_vmem()],
        out_specs=in_vmem(),
        out_shape=jax.ShapeDtypeStruct((HALF, 64, 384), jnp.bfloat16),
        scratch_shapes=[pltpu.VMEM((8, TAP_CH, 128), jnp.float32)],
        cost_estimate=pl.CostEstimate(flops=10_000_000, bytes_accessed=14_000_000, transcendentals=0),
        compiler_params=pltpu.CompilerParams(vmem_limit_bytes=16 << 20),
        name="build_taps",
    )(widths, taps)


def assemble_kernel(own_ref, x_ref, o_ref, scr):
    lane = lax.broadcasted_iota(jnp.int32, (16, 128), 1) // 16
    for bh in range(2):
        held = []
        for ri in range(2):
            for k in range(4):
                at = 256 * bh + 128 * ri
                held.append(x_ref[own_ref[k], :, at : at + 128].astype(jnp.float32))
        for k in (4, 2, 1):
            low = (lane & k) == 0
            for p in range(8):
                if p & k:
                    continue
                a, b = held[p], held[p + k]
                held[p] = jnp.where(low, a, pltpu.roll(b, 16 * k, 1))
                held[p + k] = jnp.where(low, pltpu.roll(a, 128 - 16 * k, 1), b)
        for bl in range(8):
            scr[pl.ds(8 * bh + bl, 16, stride=16), :] = held[bl]
    o_ref[...] = scr[...].reshape(16, 16, 128).astype(jnp.bfloat16)


def assemble(owner, arrived):
    return pl.pallas_call(
        assemble_kernel,
        in_specs=[in_smem(), in_vmem()],
        out_specs=in_vmem(),
        out_shape=jax.ShapeDtypeStruct((16, 16, 128), jnp.bfloat16),
        scratch_shapes=[pltpu.VMEM((256, 128), jnp.float32)],
        compiler_params=pltpu.CompilerParams(vmem_limit_bytes=16 << 20),
        name="assemble",
    )(owner, arrived)


def fold(rows):
    sub = lax.broadcasted_iota(jnp.int32, (8, 128), 0)
    for k in (4, 2, 1):
        low = (sub & k) == 0
        rows = [
            jnp.where(low, rows[i], rows[i + k])
            + jnp.where(low, pltpu.roll(rows[i], 8 - k, 0), pltpu.roll(rows[i + k], k, 0))
            for i in range(k)
        ]
    return rows[0]


def detect_kernel(count, piece_ref, t0_ref, t1_ref, x_ref, *rest):
    d_ref, b_ref, w_scr = rest[-3:]
    lane = lax.broadcasted_iota(jnp.int32, (16, 128), 1)
    inner = lane % 64
    sign = jnp.where(lane < 64, -1.0, 1.0)
    b_ref[...] = jnp.zeros_like(b_ref)

    def group(step, carry):
        for p in range(GROUP):
            source = (step * GROUP + p) * NC
            base = pl.multiple_of(piece_ref[step * GROUP + p] * NC, NC)
            sums = [[] for _ in range(4)]
            for c in range(NC):
                x = x_ref[source + c]
                slot = p * NC + c
                w_scr[slot, 0:16, :] = x
                for a in range(1, 17):
                    moved = pltpu.roll(x, a, 1)
                    w_scr[slot, 16 * a : 16 * a + 16, :] = jnp.where(inner >= a, moved, jnp.zeros_like(x))
                taps = jnp.concatenate([t0_ref[base + c, :, :272], t1_ref[base + c, :, :272]], axis=0)
                out = jnp.dot(taps, w_scr[slot], preferred_element_type=jnp.float32)
                for t in range(4):
                    real = out[32 * t : 32 * t + 16]
                    imag = out[32 * t + 16 : 32 * t + 32]
                    y = real + sign * pltpu.roll(imag, 64, 1)
                    y = y * y
                    sums[t].append(y[:8] + y[8:])
            for t in range(4):
                for g in range(0, NC, 8):
                    total = fold(sums[t][g : g + 8])
                    total = (total + pltpu.roll(total, 64, 1)) * (1.0 / DOWN)
                    d_ref[t, pl.ds(base + g, 8)] = total
                    b_ref[t] += total
        return carry

    lax.fori_loop(0, count // GROUP, group, 0)


def detect(pieces, samples, taps, earlier=None):
    n = samples.shape[0]
    in_specs = [in_smem()] + [in_vmem()] * 3
    args = [pieces, *taps, samples]
    aliases = {}
    if earlier is not None:
        in_specs.append(in_vmem())
        args.append(earlier)
        aliases = {len(args) - 1: 0}
    return pl.pallas_call(
        functools.partial(detect_kernel, n // NC),
        in_specs=in_specs,
        out_specs=[in_vmem(), in_vmem()],
        out_shape=[
            jax.ShapeDtypeStruct((4, HALF, 128), jnp.float32),
            jax.ShapeDtypeStruct((4, 8, 128), jnp.float32),
        ],
        scratch_shapes=[pltpu.VMEM((GROUP * NC, 272, 128), jnp.bfloat16)],
        input_output_aliases=aliases,
        cost_estimate=pl.CostEstimate(
            flops=n * 128 * 512 * 128 * 2, bytes_accessed=n * 128 * 384 * 2, transcendentals=0
        ),
        compiler_params=pltpu.CompilerParams(vmem_limit_bytes=16 << 20),
        name="detect",
    )(*args)


def turn_kernel(d_ref, o_ref):
    for t in range(4):
        o_ref[t] = d_ref[t].T[:64]


def turn(detected):
    return pl.pallas_call(
        turn_kernel,
        in_specs=[in_vmem()],
        out_specs=in_vmem(),
        out_shape=jax.ShapeDtypeStruct((4, 64, HALF), jnp.float32),
        compiler_params=pltpu.CompilerParams(vmem_limit_bytes=16 << 20),
        name="turn",
    )(detected)


def body(phased, filters, tap_blocks, stretch_owner):
    me = lax.axis_index("dm")
    z = me % 2
    widths = tap_blocks * BLOCK
    mine = lax.dynamic_slice_in_dim(widths, me * 2, 2)
    partner = lax.dynamic_slice_in_dim(widths, (me + 1 - 2 * z) * 2, 2)
    pieces = lax.dynamic_index_in_dim(jnp.asarray(piece_table()), me, 0, keepdims=False)

    away = lax.dynamic_slice_in_dim(filters, (1 - z) * HALF, HALF, axis=1)
    partner_taps = hop(away, 0, 0, 1)
    stay = lax.dynamic_slice_in_dim(filters, z * HALF, HALF, axis=1)

    source = lax.broadcasted_iota(jnp.int32, (256, 2, 512), 0) * 2 + lax.broadcasted_iota(jnp.int32, (256, 2, 512), 1)
    order = (source == jnp.asarray(time_order())[None, None, :]).astype(jnp.bfloat16)
    held = jnp.einsum("trc,trk->ck", phased[0], order, preferred_element_type=jnp.float32).astype(jnp.bfloat16)
    sent = held.reshape(2, DM // 2, 16, 512).transpose(1, 0, 2, 3).reshape(DM, 16, 512)
    arrived = lax.all_to_all(sent, "dm", 0, 0, tiled=True)

    near = assemble(jnp.clip(stretch_owner, 0, DM - 1), arrived)
    stay, near = lax.optimization_barrier((stay, near))
    line = [hop(near, 0, k, 0) for k in (2, 1, -1)]
    taps0 = build_taps(mine, stay)
    taps0, line = lax.optimization_barrier((taps0, line))
    taps = (taps0, build_taps(partner, partner_taps))
    row = jnp.concatenate([near, *line], axis=0)
    low, high, far = hop(row, 1, 0, 0), hop(row, -1, 0, 0), hop(row, 2, 0, 0)

    detected, bands = None, []
    for step, part in enumerate((row, low, high, far)):
        detected, band = detect(pieces[4 * step : 4 * step + 4], part, taps, detected)
        bands.append(band)

    band = jnp.sum(sum(bands), axis=1)[:, :64]
    total = band[:2] + hop(band[2:], 0, 0, 1)
    turned = turn(detected)
    total, turned = lax.optimization_barrier((total, turned))
    other = hop(turned[2:], 0, 0, 1)
    total = total + lax.ppermute(total, "chan", [(i, i ^ 1) for i in range(8)])
    total = total + lax.ppermute(total, "chan", [(i, i ^ 2) for i in range(8)])
    total, other = lax.optimization_barrier((total, other))
    total = total + lax.ppermute(total, "chan", [(i, (6 - i // 2 * 2) + i % 2) for i in range(8)])

    own = turned[:2]
    low = jnp.where(z == 0, own, other)
    high = jnp.where(z == 0, other, own)
    power = jnp.concatenate([low, high], axis=2)
    return power / (total[:, :, None] / CHANS + epsilon)


def solution(mesh):
    in_specs = (P("dm", None, None, "chan"), P("dm", "chan", None), P(), P())
    out_specs = P("dm", None, "chan")
    return jax.shard_map(body, mesh=mesh, in_specs=in_specs, out_specs=out_specs, check_vma=False)
```

```python
import functools

import jax
import jax.numpy as jnp
import numpy as np
from jax import lax
from jax.experimental import pallas as pl
from jax.experimental.pallas import tpu as pltpu
from jax.sharding import PartitionSpec as P

CHANS = 4096
BLOCK = 64
DOWN = 16
HALF = 256
NC = 16
GROUP = 4
DM = 32

epsilon = 1e-06


def place(i):
    return i // 8, (i // 2) % 4, i % 2


def index(y, x, z):
    return ((y % 4) * 4 + x % 4) * 2 + z % 2


def hop(value, dy, dx, dz):
    pairs = []
    for i in range(DM):
        y, x, z = place(i)
        pairs.append((i, index(y + dy, x + dx, z + dz)))
    return lax.ppermute(value, "dm", pairs)


def time_order():
    table = np.zeros((512,), np.int32)
    for bh in range(2):
        for ri in range(2):
            for bl in range(8):
                for m in range(16):
                    k = ((bh * 2 + ri) * 8 + bl) * 16 + m
                    table[k] = (16 * m + 15 - (8 * bh + bl)) * 2 + ri
    return table


def piece_table():
    rows = []
    for i in range(DM):
        y, x, _ = place(i)
        row = []
        for dy in (0, -1, 1, 2):
            for dx in (0, 2, -1, 1):
                row.append(4 * ((y + dy) % 4) + (x + dx) % 4)
        rows.append(row)
    return np.array(rows, np.int32)


TAP_CH = 64


def tap_kernel(live_ref, f_ref, o_ref, scr):
    lane = lax.broadcasted_iota(jnp.int32, (16, 128), 1)
    row = lax.broadcasted_iota(jnp.int32, (16, 128), 0)
    keep = lane >= row

    def group(step, carry):
        at = pl.multiple_of(step * TAP_CH, TAP_CH)
        for t in range(2):
            block = f_ref[t, pl.ds(at, TAP_CH)].astype(jnp.float32)
            tap = lax.broadcasted_iota(jnp.int32, block.shape, 1) % 256
            block = jnp.where(tap < live_ref[t], block, 0.0)
            for k in range(4):
                scr[4 * t + k] = block[:, 128 * k : 128 * k + 128]
        for t in range(2):
            for h in range(2):
                base = (t * 2 + h) * 16
                rows = slice(base, base + 16)
                for c in range(TAP_CH):
                    low = scr[4 * t + 2 * h, pl.ds(c, 16, stride=0)]
                    high = scr[4 * t + 2 * h + 1, pl.ds(c, 16, stride=0)]
                    low = pltpu.roll(low, 0, 1, stride=1, stride_axis=0)
                    high = pltpu.roll(high, 0, 1, stride=1, stride_axis=0)
                    o_ref[at + c, rows, 0:128] = jnp.where(keep, low, 0.0).astype(jnp.bfloat16)
                    o_ref[at + c, rows, 128:256] = jnp.where(keep, high, low).astype(jnp.bfloat16)
                    o_ref[at + c, rows, 256:384] = jnp.where(keep, 0.0, high).astype(jnp.bfloat16)
        return carry

    lax.fori_loop(0, HALF // TAP_CH, group, 0)


def in_vmem():
    return pl.BlockSpec(memory_space=pltpu.VMEM)


def in_smem():
    return pl.BlockSpec(memory_space=pltpu.SMEM)


def build_taps(widths, taps):
    return pl.pallas_call(
        tap_kernel,
        in_specs=[in_smem(), in_vmem()],
        out_specs=in_vmem(),
        out_shape=jax.ShapeDtypeStruct((HALF, 64, 384), jnp.bfloat16),
        scratch_shapes=[pltpu.VMEM((8, TAP_CH, 128), jnp.float32)],
        cost_estimate=pl.CostEstimate(flops=10_000_000, bytes_accessed=14_000_000, transcendentals=0),
        compiler_params=pltpu.CompilerParams(vmem_limit_bytes=16 << 20),
        name="build_taps",
    )(widths, taps)


def assemble_kernel(own_ref, x_ref, o_ref, scr):
    lane = lax.broadcasted_iota(jnp.int32, (16, 128), 1) // 16
    for bh in range(2):
        held = []
        for ri in range(2):
            for k in range(4):
                at = 256 * bh + 128 * ri
                held.append(x_ref[own_ref[k], :, at : at + 128].astype(jnp.float32))
        for k in (4, 2, 1):
            low = (lane & k) == 0
            for p in range(8):
                if p & k:
                    continue
                a, b = held[p], held[p + k]
                held[p] = jnp.where(low, a, pltpu.roll(b, 16 * k, 1))
                held[p + k] = jnp.where(low, pltpu.roll(a, 128 - 16 * k, 1), b)
        for bl in range(8):
            scr[pl.ds(8 * bh + bl, 16, stride=16), :] = held[bl]
    o_ref[...] = scr[...].reshape(16, 16, 128).astype(jnp.bfloat16)


def assemble(owner, arrived):
    return pl.pallas_call(
        assemble_kernel,
        in_specs=[in_smem(), in_vmem()],
        out_specs=in_vmem(),
        out_shape=jax.ShapeDtypeStruct((16, 16, 128), jnp.bfloat16),
        scratch_shapes=[pltpu.VMEM((256, 128), jnp.float32)],
        compiler_params=pltpu.CompilerParams(vmem_limit_bytes=16 << 20),
        name="assemble",
    )(owner, arrived)


def fold(rows):
    sub = lax.broadcasted_iota(jnp.int32, (8, 128), 0)
    for k in (4, 2, 1):
        low = (sub & k) == 0
        rows = [
            jnp.where(low, rows[i], rows[i + k])
            + jnp.where(low, pltpu.roll(rows[i], 8 - k, 0), pltpu.roll(rows[i + k], k, 0))
            for i in range(k)
        ]
    return rows[0]


def detect_kernel(count, piece_ref, t0_ref, t1_ref, x_ref, *rest):
    d_ref, b_ref, w_scr = rest[-3:]
    lane = lax.broadcasted_iota(jnp.int32, (16, 128), 1)
    inner = lane % 64
    sign = jnp.where(lane < 64, -1.0, 1.0)
    b_ref[...] = jnp.zeros_like(b_ref)

    def group(step, carry):
        for p in range(GROUP):
            source = (step * GROUP + p) * NC
            base = pl.multiple_of(piece_ref[step * GROUP + p] * NC, NC)
            sums = [[] for _ in range(4)]
            for c in range(NC):
                x = x_ref[source + c]
                slot = p * NC + c
                w_scr[slot, 0:16, :] = x
                for a in range(1, 17):
                    moved = pltpu.roll(x, a, 1)
                    w_scr[slot, 16 * a : 16 * a + 16, :] = jnp.where(inner >= a, moved, jnp.zeros_like(x))
                taps = jnp.concatenate([t0_ref[base + c, :, :272], t1_ref[base + c, :, :272]], axis=0)
                out = jnp.dot(taps, w_scr[slot], preferred_element_type=jnp.float32)
                for t in range(4):
                    real = out[32 * t : 32 * t + 16]
                    imag = out[32 * t + 16 : 32 * t + 32]
                    y = real + sign * pltpu.roll(imag, 64, 1)
                    y = y * y
                    sums[t].append(y[:8] + y[8:])
            for t in range(4):
                for g in range(0, NC, 8):
                    total = fold(sums[t][g : g + 8])
                    total = (total + pltpu.roll(total, 64, 1)) * (1.0 / DOWN)
                    d_ref[t, pl.ds(base + g, 8)] = total
                    b_ref[t] += total
        return carry

    lax.fori_loop(0, count // GROUP, group, 0)


def detect(pieces, samples, taps, earlier=None):
    n = samples.shape[0]
    in_specs = [in_smem()] + [in_vmem()] * 3
    args = [pieces, *taps, samples]
    aliases = {}
    if earlier is not None:
        in_specs.append(in_vmem())
        args.append(earlier)
        aliases = {len(args) - 1: 0}
    return pl.pallas_call(
        functools.partial(detect_kernel, n // NC),
        in_specs=in_specs,
        out_specs=[in_vmem(), in_vmem()],
        out_shape=[
            jax.ShapeDtypeStruct((4, HALF, 128), jnp.float32),
            jax.ShapeDtypeStruct((4, 8, 128), jnp.float32),
        ],
        scratch_shapes=[pltpu.VMEM((GROUP * NC, 272, 128), jnp.bfloat16)],
        input_output_aliases=aliases,
        cost_estimate=pl.CostEstimate(
            flops=n * 128 * 512 * 128 * 2, bytes_accessed=n * 128 * 384 * 2, transcendentals=0
        ),
        compiler_params=pltpu.CompilerParams(vmem_limit_bytes=16 << 20),
        name="detect",
    )(*args)


def turn_kernel(d_ref, o_ref):
    for t in range(4):
        o_ref[t] = d_ref[t].T[:64]


def turn(detected):
    return pl.pallas_call(
        turn_kernel,
        in_specs=[in_vmem()],
        out_specs=in_vmem(),
        out_shape=jax.ShapeDtypeStruct((4, 64, HALF), jnp.float32),
        compiler_params=pltpu.CompilerParams(vmem_limit_bytes=16 << 20),
        name="turn",
    )(detected)


def body(phased, filters, tap_blocks, stretch_owner):
    me = lax.axis_index("dm")
    z = me % 2
    widths = tap_blocks * BLOCK
    mine = lax.dynamic_slice_in_dim(widths, me * 2, 2)
    partner = lax.dynamic_slice_in_dim(widths, (me + 1 - 2 * z) * 2, 2)
    pieces = lax.dynamic_index_in_dim(jnp.asarray(piece_table()), me, 0, keepdims=False)

    away = lax.dynamic_slice_in_dim(filters, (1 - z) * HALF, HALF, axis=1)
    partner_taps = hop(away, 0, 0, 1)
    stay = lax.dynamic_slice_in_dim(filters, z * HALF, HALF, axis=1)

    source = lax.broadcasted_iota(jnp.int32, (256, 2, 512), 0) * 2 + lax.broadcasted_iota(jnp.int32, (256, 2, 512), 1)
    order = (source == jnp.asarray(time_order())[None, None, :]).astype(jnp.bfloat16)
    held = jnp.einsum("trc,trk->ck", phased[0], order, preferred_element_type=jnp.float32).astype(jnp.bfloat16)
    sent = held.reshape(2, DM // 2, 16, 512).transpose(1, 0, 2, 3).reshape(DM, 16, 512)
    arrived = lax.all_to_all(sent, "dm", 0, 0, tiled=True)

    near = assemble(jnp.clip(stretch_owner, 0, DM - 1), arrived)
    stay, near = lax.optimization_barrier((stay, near))
    line = [hop(near, 0, k, 0) for k in (2, 1, -1)]
    taps0 = build_taps(mine, stay)
    taps0, line = lax.optimization_barrier((taps0, line))
    taps = (taps0, build_taps(partner, partner_taps))
    row = jnp.concatenate([near, *line], axis=0)
    low, high, far = hop(row, 1, 0, 0), hop(row, -1, 0, 0), hop(row, 2, 0, 0)

    detected, bands = None, []
    for step, part in enumerate((row, low, high, far)):
        detected, band = detect(pieces[4 * step : 4 * step + 4], part, taps, detected)
        bands.append(band)

    band = jnp.sum(sum(bands), axis=1)[:, :64]
    total = band[:2] + hop(band[2:], 0, 0, 1)
    turned = turn(detected)
    total, turned = lax.optimization_barrier((total, turned))
    other = hop(turned[2:], 0, 0, 1)
    total = total + lax.ppermute(total, "chan", [(i, i ^ 1) for i in range(8)])
    total = total + lax.ppermute(total, "chan", [(i, i ^ 2) for i in range(8)])
    total, other = lax.optimization_barrier((total, other))
    total = total + lax.ppermute(total, "chan", [(i, (6 - i // 2 * 2) + i % 2) for i in range(8)])

    own = turned[:2]
    low = jnp.where(z == 0, own, other)
    high = jnp.where(z == 0, other, own)
    power = jnp.concatenate([low, high], axis=2)
    return power / (total[:, :, None] / CHANS + epsilon)


def solution(mesh):
    in_specs = (P("dm", None, None, "chan"), P("dm", "chan", None), P(), P())
    out_specs = P("dm", None, "chan")
    return jax.shard_map(body, mesh=mesh, in_specs=in_specs, out_specs=out_specs, check_vma=False)
```
